32 devices in a mesh: dp: 2 (over y), seq: 16 (over z, x, core).
Axes of the slice: x: 2, y: 2, z: 4, core: 2. Of those that a mesh axis runs over, the one named last changes fastest.
Arguments:
- q_img: bfloat16 [2, 2048, 2048], P('dp', 'seq'), may hold values from -6 to 6
- k_img: bfloat16 [2, 2048, 2048], P('dp', 'seq'), may hold values from -6 to 6
- v_img: bfloat16 [2, 2048, 2048], P('dp', 'seq'), may hold values from -12 to 12
- x_txt: bfloat16 [2, 77, 2432], P('dp'), may hold values from -9 to 9
- w_txt: bfloat16 [3, 2432, 2048], P(None, 'dp', 'seq'), may hold values from -0.125 to 0.125
- grad_img: bfloat16 [2, 2048, 2048], P('dp', 'seq'), may hold values from -6 to 6
- grad_txt: bfloat16 [2, 77, 2048], P('dp', None, 'seq'), may hold values from -6 to 6
Outputs:
- o_img: bfloat16 [2, 2048, 2048], P('dp', 'seq')
- o_txt: bfloat16 [2, 77, 2048], P('dp', None, 'seq')
- grad_qkv_img: bfloat16 [3, 2, 2048, 2048], P(None, 'dp', 'seq')
- dx_txt: float32 [2, 77, 2432], P('dp', None, 'seq')
- dw_txt: float32 [3, 2432, 2048], P(None, 'dp', 'seq')
The draws below stay inside these ranges and needn't reach their ends.
All inputs are finite; a program needn't handle non-finite values.
Results may differ from the reference program's by a relative error of at most 0.014.
Values may be sent and summed in bfloat16 or wider, within the bound.
A program may use at most 64 MiB of HBM per device.

```python
import math
import jax
import jax.numpy as jnp
from jax import lax

D = 2432
HEADS = 32
HEAD_DIM = 64
TXT = 77
HD = 2048
IMG = 2048
SAMPLES = 2


def draw_q_img(key, part):
    base = jnp.clip(1.5 * jax.random.normal(jax.random.fold_in(key, 1), (SAMPLES, IMG, HD), jnp.float32), -6.0, 6.0)
    return base.astype(jnp.bfloat16)


def draw_k_img(key, part):
    base = jnp.clip(1.5 * jax.random.normal(jax.random.fold_in(key, 2), (SAMPLES, IMG, HD), jnp.float32), -6.0, 6.0)
    return base.astype(jnp.bfloat16)


def levels(stream_key, extent, split, smallest, largest):
    factor_of = 1.0
    for position, parts in split:
        heights = jax.random.uniform(jax.random.fold_in(jax.random.fold_in(stream_key, 6), position), (parts,), jnp.float32, smallest / len(split), largest / len(split))
        factor_of = factor_of * jnp.repeat(jnp.exp(heights), extent[position] // parts).reshape((-1,) + (1,) * (len(extent) - 1 - position))
    return factor_of


def gaussian(stream_key, dims, spread, reach, pieces=(), held_as=jnp.bfloat16):
    loudness = levels(stream_key, dims, pieces, -0.22, 0.18) if pieces else 1.0
    result = jax.random.normal(stream_key, dims, jnp.float32) * spread * loudness
    return jnp.minimum(jnp.maximum(result, -reach), reach).astype(held_as)


def setup_inputs(seed: int = 0) -> dict:
    streams_of = jax.random.split(jax.random.key(seed), 8)
    return {
        "q_img": draw_q_img(jax.random.fold_in(streams_of[7], 71), 0),
        "k_img": draw_k_img(jax.random.fold_in(streams_of[7], 71), 0),
        "v_img": gaussian(streams_of[2], (SAMPLES, IMG, HD), 2.0, 12.0, ((0, 2), (1, 16))),
        "x_txt": gaussian(streams_of[3], (SAMPLES, TXT, D), 1.5, 9.0, ((0, 2),)),
        "w_txt": gaussian(streams_of[4], (3, D, HD), D ** -0.5, 0.125, ((1, 2), (2, 16))),
        "grad_img": gaussian(streams_of[5], (SAMPLES, IMG, HD), 1.0, 6.0, ((0, 2), (1, 16))),
        "grad_txt": gaussian(streams_of[6], (SAMPLES, TXT, HD), 1.0, 6.0, ((0, 2), (2, 16))),
    }


def attend(query, keys, values, cotangent):
    scale = 1.0 / math.sqrt(HEAD_DIM)
    scores = jnp.dot(query, keys.T, preferred_element_type=jnp.float32) * scale
    shifted = jnp.exp(scores - lax.optimization_barrier(jnp.max(scores, axis=1, keepdims=True)))
    probs = shifted / lax.optimization_barrier(jnp.sum(shifted, axis=1, keepdims=True))
    probs_b = probs.astype(jnp.bfloat16)
    joint_o = jnp.dot(probs_b, values, preferred_element_type=jnp.float32).astype(jnp.bfloat16)
    value_grads = jnp.dot(probs_b.T, cotangent, preferred_element_type=jnp.float32).astype(jnp.bfloat16)
    prob_grads = jnp.dot(cotangent, values.T, preferred_element_type=jnp.float32)
    row_terms = lax.optimization_barrier(jnp.sum(cotangent.astype(jnp.float32) * joint_o.astype(jnp.float32), axis=1, keepdims=True))
    score_grads = (probs * (prob_grads - row_terms)).astype(jnp.bfloat16)
    query_grads = (jnp.dot(score_grads, keys, preferred_element_type=jnp.float32) * scale).astype(jnp.bfloat16)
    key_grads = (jnp.dot(score_grads.T, query, preferred_element_type=jnp.float32) * scale).astype(jnp.bfloat16)
    return (joint_o, query_grads, key_grads, value_grads)

def reference(q_img, k_img, v_img, x_txt, w_txt, grad_img, grad_txt):
    text_qkv = jnp.einsum('std,idh->isth', x_txt.astype(jnp.float32), w_txt.astype(jnp.float32)).astype(jnp.bfloat16)
    length = IMG + TXT

    def to_heads(image_part, text_part):
        whole = jnp.concatenate([image_part, text_part], axis=1)
        whole = whole.reshape(SAMPLES, length, HEADS, HEAD_DIM).transpose(0, 2, 1, 3)
        return whole.reshape(SAMPLES * HEADS, length, HEAD_DIM)

    def from_heads(stacked):
        whole = stacked.reshape(SAMPLES, HEADS, length, HEAD_DIM).transpose(0, 2, 1, 3).reshape(SAMPLES, length, HD)
        return (whole[:, :IMG], whole[:, IMG:])
    inputs = (to_heads(q_img, text_qkv[0]), to_heads(k_img, text_qkv[1]), to_heads(v_img, text_qkv[2]), to_heads(grad_img, grad_txt))
    joint_o, query_grads, key_grads, value_grads = lax.map(lambda items: attend(*items), inputs)
    o_img, o_txt = from_heads(joint_o)
    dq_image, dq_text = from_heads(query_grads)
    dk_image, dk_text = from_heads(key_grads)
    dv_image, dv_text = from_heads(value_grads)
    grad_qkv_img = jnp.stack([dq_image, dk_image, dv_image])
    text_grads = jnp.stack([dq_text, dk_text, dv_text])
    dw_txt = jnp.einsum('std,isth->idh', x_txt.astype(jnp.float32), text_grads.astype(jnp.float32))
    dx_txt = jnp.einsum('isth,idh->std', text_grads.astype(jnp.float32), w_txt.astype(jnp.float32))
    return (o_img, o_txt, grad_qkv_img, dx_txt, dw_txt)
```

```python
import functools
import math

import jax
import jax.numpy as jnp
from jax import lax
from jax.experimental import pallas as pl
from jax.experimental.pallas import tpu as pltpu
from jax.sharding import PartitionSpec as P

HEAD_DIM = 64
BF = jnp.bfloat16
F32 = jnp.float32
NT = (((1,), (1,)), ((), ()))
TN = (((0,), (0,)), ((), ()))


def up(value, step):
    return (value + step - 1) // step * step


def dotf(a, b, dims=(((1,), (0,)), ((), ()))):
    return lax.dot_general(a, b, dims, preferred_element_type=F32)


def kernel(
    cfg,
    q_in, k_in, v_in, g_in, x_in, w_ref, gt_ref,
    o_out, gr_out, ot_out, dx_out, dw_out,
    kbuf, vbuf, qbuf, gbuf, xall, part, partl, kaug, kh, vaug, vh, pbuf, sbuf, gst, qst,
    obuf, dqbuf, dkacc, dvacc, dkb, dvb, tg, tgl, dxs, dxl,
    in_send, in_recv, out_send, out_recv, xs_sem, xr_sem, ps_sem, pr_sem, ts_sem, tr_sem,
    ds_sem, dr_sem, loc_sem,
):
    n, ndp, rows, cols, txt, tsub, tkey, dloc, dblk, group = cfg
    heads = cols // HEAD_DIM
    img = n * rows
    length = img + tkey
    m = group * rows
    steps = n // group
    nb = dloc // dblk
    me = lax.axis_index("seq")
    dp = lax.axis_index("dp")
    wide = cols % 128 == 0

    def tile(ref, j):
        if wide:
            return ref.at[:, pl.ds(pl.multiple_of(j * cols, 128), cols)]
        return ref.at[j]

    def at_rows(ref, j):
        return ref.at[pl.ds(pl.multiple_of(j * rows, 16), rows), :]

    barrier = pltpu.get_barrier_semaphore()
    total = n * ndp

    def greet(i, c):
        flat = lax.rem(dp * n + me + i, total)
        pl.semaphore_signal(
            barrier, inc=1, device_id={"dp": flat // n, "seq": lax.rem(flat, n)},
            device_id_type=pl.DeviceIdType.MESH,
        )
        return c

    lax.fori_loop(1, total, greet, 0)
    pl.semaphore_wait(barrier, total - 1)

    ins = (k_in, v_in, q_in, g_in)
    bufs = (kbuf, vbuf, qbuf, gbuf)

    def in_copy(a, dest, source):
        return pltpu.make_async_remote_copy(
            src_ref=tile(ins[a], dest), dst_ref=at_rows(bufs[a], source),
            send_sem=in_send.at[a, dest], recv_sem=in_recv.at[a, source],
            device_id={"seq": dest}, device_id_type=pl.DeviceIdType.MESH,
        )

    def own_copy(a):
        return pltpu.make_async_copy(tile(ins[a], me), at_rows(bufs[a], me), loc_sem.at[a])

    def x_copy(p, source):
        return pltpu.make_async_remote_copy(
            src_ref=x_in.at[p], dst_ref=xall.at[source],
            send_sem=xs_sem.at[p], recv_sem=xr_sem.at[source],
            device_id={"dp": p}, device_id_type=pl.DeviceIdType.MESH,
        )

    def p_copy(p, source):
        return pltpu.make_async_remote_copy(
            src_ref=part.at[p], dst_ref=partl.at[source],
            send_sem=ps_sem.at[p], recv_sem=pr_sem.at[source],
            device_id={"dp": p}, device_id_type=pl.DeviceIdType.MESH,
        )

    def t_copy(p, source):
        return pltpu.make_async_remote_copy(
            src_ref=tg, dst_ref=tgl.at[source],
            send_sem=ts_sem.at[p], recv_sem=tr_sem.at[source],
            device_id={"dp": p}, device_id_type=pl.DeviceIdType.MESH,
        )

    own_x = pltpu.make_async_copy(x_in.at[dp], xall.at[dp], loc_sem.at[4])
    own_x.start()
    for i in range(1, ndp):
        x_copy(lax.rem(dp + i, ndp), dp).start()

    def send_kv(i, c):
        dest = lax.rem(me + i, n)
        in_copy(0, dest, me).start()
        in_copy(1, dest, me).start()
        return c

    lax.fori_loop(1, n, send_kv, 0)
    for a in range(4):
        own_copy(a).start()
    my_group = me // group

    def send_qg(t, c):
        for e in range(group):
            dest = lax.rem(my_group + steps - t, steps) * group + e

            @pl.when(dest != me)
            def _():
                in_copy(2, dest, me).start()
                in_copy(3, dest, me).start()

        return c

    lax.fori_loop(0, steps, send_qg, 0)

    own_x.wait()
    for i in range(ndp):
        s = lax.rem(dp + i, ndp)
        if i:
            x_copy(dp, s).wait_recv()
        for j in range(3):
            product = dotf(xall[s], w_ref[j])
            if i:
                part[s, j] = product
            else:
                partl[dp, j] = product
        if i:
            p_copy(s, dp).start()
    for i in range(1, ndp):
        p_copy(dp, lax.rem(dp + i, ndp)).wait_recv()
    for j, buf in enumerate((qbuf, kbuf, vbuf)):
        value = partl[0, j]
        for s in range(1, ndp):
            value = value + partl[s, j]
        buf[pl.ds(img, tsub), :] = value.astype(BF)
        pad = buf.shape[0] - img - tsub
        buf[pl.ds(img + tsub, pad), :] = jnp.zeros((pad, cols), BF)
    gbuf[pl.ds(img, tsub), :] = gt_ref[...]
    pad = gbuf.shape[0] - img - tsub
    gbuf[pl.ds(img + tsub, pad), :] = jnp.zeros((pad, cols), BF)
    dkacc[...] = jnp.zeros_like(dkacc)
    dvacc[...] = jnp.zeros_like(dvacc)

    def wait_kv(i, c):
        source = lax.rem(me + i, n)
        in_copy(0, me, source).wait_recv()
        in_copy(1, me, source).wait_recv()
        return c

    lax.fori_loop(1, n, wait_kv, 0)
    for a in range(4):
        own_copy(a).wait()

    lane_head = lax.broadcasted_iota(jnp.int32, (m, cols), 1) // HEAD_DIM

    def build(r, c):
        at = pl.ds(pl.multiple_of(r * 128, 128), 128)
        lane = lax.broadcasted_iota(jnp.int32, (128, cols), 1)
        row = lax.broadcasted_iota(jnp.int32, (128, cols), 0) + r * 128
        kk = kbuf[at, :]
        vv = vbuf[at, :]
        bias = jnp.where((row >= img + txt) & (lane == 0), -1e30, 0.0).astype(BF)
        ones = jnp.ones((128, cols), BF)
        zero = jnp.zeros((128, cols), BF)
        kaug[at, :] = jnp.concatenate([kk, bias], axis=1)
        vaug[at, :] = jnp.concatenate([vv, ones], axis=1)
        for h in range(heads):
            mine = lane // HEAD_DIM == h
            kh[h, at, :] = jnp.where(mine, kk, zero)
            vh[h, at, :] = jnp.concatenate(
                [jnp.where(mine, vv, zero), jnp.where(mine, ones, zero)], axis=1
            )
        return c

    lax.fori_loop(0, length // 128, build, 0)
    scale = 1.0 / math.sqrt(HEAD_DIM)

    def out_copy(a, dest, source):
        send = (obuf, dqbuf, dkb, dvb)[a]
        land = o_out if a == 0 else gr_out.at[a - 1]
        return pltpu.make_async_remote_copy(
            src_ref=at_rows(send, dest), dst_ref=tile(land, source),
            send_sem=out_send.at[a, dest], recv_sem=out_recv.at[a, source],
            device_id={"seq": dest}, device_id_type=pl.DeviceIdType.MESH,
        )

    def own_out(a):
        send = (obuf, dqbuf, dkb, dvb)[a]
        land = o_out if a == 0 else gr_out.at[a - 1]
        return pltpu.make_async_copy(at_rows(send, me), tile(land, me), loc_sem.at[5 + a])

    def step(t, c):
        which = lax.rem(my_group + t + steps - 1, steps)
        first = jnp.where(t == 0, img, which * m)
        for e in range(group):
            source = which * group + e

            @pl.when((t > 0) & (source != me))
            def _():
                in_copy(2, me, source).wait_recv()
                in_copy(3, me, source).wait_recv()

        at = pl.ds(pl.multiple_of(first, 128), m)
        qs = qbuf[at, :] * jnp.asarray(scale, BF)
        g = gbuf[at, :].astype(F32)
        zero = jnp.zeros_like(qs)
        one = jnp.where(lax.broadcasted_iota(jnp.int32, (m, cols), 1) == 0, 1.0, 0.0).astype(BF)
        acc = jnp.zeros((m, 2 * cols), F32)
        for h in range(heads):
            qm = jnp.where(lane_head == h, qs, zero)
            qst[pl.ds(h * m, m), :] = qm
            scores = dotf(jnp.concatenate([qm, one], axis=1), kaug[...], NT)
            top = jnp.max(scores, axis=1, keepdims=True)
            p = jnp.exp(scores - top).astype(BF)
            pbuf[pl.ds(h * m, m), :] = p
            acc = acc + dotf(p, vh[h])
        inverse = 1.0 / acc[:, cols:]
        ob = (acc[:, :cols] * inverse).astype(BF)
        gp = (g * inverse).astype(BF)
        term = -(ob.astype(F32) * gp.astype(F32)).astype(BF)
        dq = jnp.zeros((m, cols), F32)
        for h in range(heads):
            gm = jnp.where(lane_head == h, gp, zero)
            gst[pl.ds(h * m, m), :] = gm
            lhs = jnp.concatenate([gm, jnp.where(lane_head == h, term, zero)], axis=1)
            inner = dotf(lhs, vaug[...], NT)
            ds = inner.astype(BF) * pbuf[pl.ds(h * m, m), :]
            sbuf[pl.ds(h * m, m), :] = ds
            dq = dq + dotf(ds, kh[h])
        obuf[at, :] = ob
        dqbuf[at, :] = (dq * scale).astype(BF)
        for e in range(group):
            dest = which * group + e

            @pl.when((t > 0) & (dest != me))
            def _():
                out_copy(0, dest, me).start()
                out_copy(1, dest, me).start()

            @pl.when((t > 0) & (dest == me))
            def _():
                own_out(0).start()
                own_out(1).start()

        dvacc[...] += dotf(pbuf[...], gst[...], TN)
        dkacc[...] += dotf(sbuf[...], qst[...], TN)
        return c

    lax.fori_loop(0, steps + 1, step, 0)

    text = pl.ds(img, tsub)
    tg[0] = dqbuf[text, :]
    tg[1] = dkacc[text, :].astype(BF)
    tg[2] = dvacc[text, :].astype(BF)
    for i in range(1, ndp):
        t_copy(lax.rem(dp + i, ndp), dp).start()
    ot_out[...] = obuf[text, :]

    def send_dkv(i, c):
        dest = lax.rem(me + i, n)
        at = pl.ds(pl.multiple_of(dest * rows, 16), rows)
        dkb[at, :] = dkacc[at, :].astype(BF)
        dvb[at, :] = dvacc[at, :].astype(BF)

        @pl.when(dest != me)
        def _():
            out_copy(2, dest, me).start()
            out_copy(3, dest, me).start()

        @pl.when(dest == me)
        def _():
            own_out(2).start()
            own_out(3).start()

        return c

    lax.fori_loop(1, n + 1, send_dkv, 0)

    tgl[dp] = tg[...]
    for i in range(1, ndp):
        t_copy(dp, lax.rem(dp + i, ndp)).wait_recv()

    def dx_copy(s, b, source):
        return pltpu.make_async_remote_copy(
            src_ref=dxs.at[s, b], dst_ref=dxl.at[source],
            send_sem=ds_sem.at[s, b], recv_sem=dr_sem.at[source],
            device_id={"dp": s, "seq": dp * nb + b}, device_id_type=pl.DeviceIdType.MESH,
        )

    for s in range(ndp):
        value = dotf(tgl[s, 0], w_ref[0], NT)
        for j in range(1, 3):
            value = value + dotf(tgl[s, j], w_ref[j], NT)
        for b in range(nb):
            dxs[s, b] = value[:, b * dblk:(b + 1) * dblk].astype(BF)
        for b in range(nb):
            mine = (dp == s) & (dp * nb + b == me)

            @pl.when(jnp.logical_not(mine))
            def _():
                dx_copy(s, b, me).start()

            @pl.when(mine)
            def _():
                pltpu.make_async_copy(dxs.at[s, b], dxl.at[me], dr_sem.at[me]).start()

    for j in range(3):
        value = dotf(xall[0], tgl[0, j], TN)
        for s in range(1, ndp):
            value = value + dotf(xall[s], tgl[s, j], TN)
        dw_out[j] = value

    holder = me // nb
    own_dx = holder == dp

    def wait_dx(r, c):
        @pl.when(jnp.logical_not(own_dx & (r == me)))
        def _():
            dx_copy(0, 0, r).wait_recv()

        @pl.when(own_dx & (r == me))
        def _():
            pltpu.make_async_copy(dxs.at[0, 0], dxl.at[r], dr_sem.at[r]).wait()

        return c

    lax.fori_loop(0, n, wait_dx, 0)
    sums = dxl[0].astype(F32)
    for r in range(1, n):
        sums = sums + dxl[r].astype(F32)
    dx_out[...] = sums

    for a in range(4):
        own_out(a).wait()

    def drain(i, c):
        other = lax.rem(me + i, n)
        for a in range(4):
            out_copy(a, me, other).wait_recv()
            out_copy(a, other, me).wait_send()
            in_copy(a, other, me).wait_send()
        return c

    lax.fori_loop(1, n, drain, 0)
    for i in range(1, ndp):
        p = lax.rem(dp + i, ndp)
        x_copy(p, dp).wait_send()
        p_copy(p, dp).wait_send()
        t_copy(p, dp).wait_send()
    for s in range(ndp):
        for b in range(nb):

            @pl.when(jnp.logical_not((dp == s) & (dp * nb + b == me)))
            def _():
                dx_copy(s, b, me).wait_send()


def local(n, ndp, q_img, k_img, v_img, x_txt, w_txt, grad_img, grad_txt):
    _, rows, hd = q_img.shape
    cols = hd // n
    heads = cols // HEAD_DIM
    txt, width = x_txt.shape[1:]
    dloc = w_txt.shape[1]
    dblk = width // n
    tsub = up(txt, 16)
    tkey = up(txt, 128)
    group = 2
    m = group * rows
    nb = dloc // dblk
    length = n * rows + tkey
    qlen = n * rows + m
    wide = cols % 128 == 0

    def spread(a):
        return a[0] if wide else a[0].reshape(rows, n, cols).transpose(1, 0, 2)

    x_parts = jnp.pad(x_txt[0], ((0, tsub - txt), (0, 0)))
    x_parts = x_parts.reshape(tsub, ndp, dloc).transpose(1, 0, 2)
    gt = jnp.pad(grad_txt[0], ((0, tsub - txt), (0, 0)))
    shape = (rows, hd) if wide else (n, rows, cols)
    hbm = pl.BlockSpec(memory_space=pl.ANY)
    vmem = pl.BlockSpec(memory_space=pltpu.VMEM)
    cfg = (n, ndp, rows, cols, txt, tsub, tkey, dloc, dblk, group)
    dma = pltpu.SemaphoreType.DMA
    o, gr, ot, dx, dw = pl.pallas_call(
        functools.partial(kernel, cfg),
        out_shape=(
            jax.ShapeDtypeStruct(shape, BF),
            jax.ShapeDtypeStruct((3,) + shape, BF),
            jax.ShapeDtypeStruct((tsub, cols), BF),
            jax.ShapeDtypeStruct((tsub, dblk), F32),
            jax.ShapeDtypeStruct((3, dloc, cols), F32),
        ),
        in_specs=[hbm] * 5 + [vmem] * 2,
        out_specs=(hbm, hbm, vmem, vmem, vmem),
        scratch_shapes=[
            pltpu.VMEM((length, cols), BF),
            pltpu.VMEM((length, cols), BF),
            pltpu.VMEM((qlen, cols), BF),
            pltpu.VMEM((qlen, cols), BF),
            pltpu.VMEM((ndp, tsub, dloc), BF),
            pltpu.VMEM((ndp, 3, tsub, cols), F32),
            pltpu.VMEM((ndp, 3, tsub, cols), F32),
            pltpu.VMEM((length, 2 * cols), BF),
            pltpu.VMEM((heads, length, cols), BF),
            pltpu.VMEM((length, 2 * cols), BF),
            pltpu.VMEM((heads, length, 2 * cols), BF),
            pltpu.VMEM((heads * m, length), BF),
            pltpu.VMEM((heads * m, length), BF),
            pltpu.VMEM((heads * m, cols), BF),
            pltpu.VMEM((heads * m, cols), BF),
            pltpu.VMEM((qlen, cols), BF),
            pltpu.VMEM((qlen, cols), BF),
            pltpu.VMEM((length, cols), F32),
            pltpu.VMEM((length, cols), F32),
            pltpu.VMEM((length, cols), BF),
            pltpu.VMEM((length, cols), BF),
            pltpu.VMEM((3, tsub, cols), BF),
            pltpu.VMEM((ndp, 3, tsub, cols), BF),
            pltpu.VMEM((ndp, nb, tsub, dblk), BF),
            pltpu.VMEM((n, tsub, dblk), BF),
            dma((4, n)), dma((4, n)), dma((4, n)), dma((4, n)),
            dma((ndp,)), dma((ndp,)), dma((ndp,)), dma((ndp,)), dma((ndp,)), dma((ndp,)),
            dma((ndp, nb)), dma((n,)), dma((9,)),
        ],
        compiler_params=pltpu.CompilerParams(
            collective_id=0, has_side_effects=True, vmem_limit_bytes=60 * 1024 * 1024
        ),
    )(spread(q_img), spread(k_img), spread(v_img), spread(grad_img), x_parts, w_txt, gt)
    if not wide:
        o = o.transpose(1, 0, 2).reshape(rows, hd)
        gr = gr.transpose(0, 2, 1, 3).reshape(3, rows, hd)
    return (o[None], ot[None, :txt], gr[:, None], dx[None, :txt], dw)


def solution(mesh):
    n, ndp = mesh.shape["seq"], mesh.shape["dp"]
    in_specs = (
        P("dp", "seq", None),
        P("dp", "seq", None),
        P("dp", "seq", None),
        P("dp", None, None),
        P(None, "dp", "seq"),
        P("dp", "seq", None),
        P("dp", None, "seq"),
    )
    out_specs = (
        P("dp", "seq", None),
        P("dp", None, "seq"),
        P(None, "dp", "seq", None),
        P("dp", None, "seq"),
        P(None, "dp", "seq"),
    )
    return jax.shard_map(
        functools.partial(local, n, ndp), mesh=mesh, in_specs=in_specs, out_specs=out_specs,
        check_vma=False,
    )
```

```python
import functools
import math

import jax
import jax.numpy as jnp
from jax import lax
from jax.experimental import pallas as pl
from jax.experimental.pallas import tpu as pltpu
from jax.sharding import PartitionSpec as P

HEAD_DIM = 64
QUAD = 4
BF = jnp.bfloat16
F32 = jnp.float32
NT = (((1,), (1,)), ((), ()))
TN = (((0,), (0,)), ((), ()))


def up(value, step):
    return (value + step - 1) // step * step


def dotf(a, b, dims=(((1,), (0,)), ((), ()))):
    return lax.dot_general(a, b, dims, preferred_element_type=F32)


def kernel(
    cfg,
    q_in, k_in, v_in, g_in, x_ref, w_ref, gt_ref,
    o_out, gr_out, ot_out, dx_out, x_out, tg_out,
    kbuf, vbuf, qbuf, gbuf, xall, part, partl, kaug, kh, vaug, vh, pbuf, sbuf, gst, qst,
    obuf, dqbuf, dkacc, dvacc, dkb, dvb, tg, tgl, dxs, dx1, dx2, dxl,
    xf, gf, xs,
    in_send, in_recv, out_send, out_recv, xs_sem, xr_sem, ps_sem, pr_sem, ts_sem, tr_sem,
    d1s_sem, d1r_sem, ds_sem, dr_sem, loc_sem,
):
    n, ndp, rows, cols, txt, tsub, tkey, dloc, dblk, group = cfg
    heads = cols // HEAD_DIM
    img = n * rows
    length = img + tkey
    m = group * rows
    steps = n // group
    nb = dloc // dblk
    me = lax.axis_index("seq")
    dp = lax.axis_index("dp")
    wide = cols % 128 == 0

    def tile(ref, j):
        if wide:
            return ref.at[:, pl.ds(pl.multiple_of(j * cols, 128), cols)]
        return ref.at[j]

    def at_rows(ref, j):
        return ref.at[pl.ds(pl.multiple_of(j * rows, 16), rows), :]

    barrier = pltpu.get_barrier_semaphore()
    total = n * ndp

    def greet(i, c):
        flat = lax.rem(dp * n + me + i, total)
        pl.semaphore_signal(
            barrier, inc=1, device_id={"dp": flat // n, "seq": lax.rem(flat, n)},
            device_id_type=pl.DeviceIdType.MESH,
        )
        return c

    lax.fori_loop(1, total, greet, 0)
    pl.semaphore_wait(barrier, total - 1)

    ins = (k_in, v_in, q_in, g_in)
    bufs = (kbuf, vbuf, qbuf, gbuf)

    def in_copy(a, dest, source):
        return pltpu.make_async_remote_copy(
            src_ref=tile(ins[a], dest), dst_ref=at_rows(bufs[a], source),
            send_sem=in_send.at[a, dest], recv_sem=in_recv.at[a, source],
            device_id={"seq": dest}, device_id_type=pl.DeviceIdType.MESH,
        )

    def own_copy(a):
        return pltpu.make_async_copy(tile(ins[a], me), at_rows(bufs[a], me), loc_sem.at[a])

    def x_copy(p, source):
        return pltpu.make_async_remote_copy(
            src_ref=xs.at[p], dst_ref=xall.at[source],
            send_sem=xs_sem.at[p], recv_sem=xr_sem.at[source],
            device_id={"dp": p}, device_id_type=pl.DeviceIdType.MESH,
        )

    def p_copy(p, source):
        return pltpu.make_async_remote_copy(
            src_ref=part.at[p], dst_ref=partl.at[source],
            send_sem=ps_sem.at[p], recv_sem=pr_sem.at[source],
            device_id={"dp": p}, device_id_type=pl.DeviceIdType.MESH,
        )

    def t_copy(p, source):
        return pltpu.make_async_remote_copy(
            src_ref=tg, dst_ref=tgl.at[source],
            send_sem=ts_sem.at[p], recv_sem=tr_sem.at[source],
            device_id={"dp": p}, device_id_type=pl.DeviceIdType.MESH,
        )

    def send_kv(i, c):
        dest = lax.rem(me + i, n)
        in_copy(0, dest, me).start()
        in_copy(1, dest, me).start()
        return c

    lax.fori_loop(1, n, send_kv, 0)
    for a in range(4):
        own_copy(a).start()
    my_group = me // group

    def send_qg(t, c):
        for e in range(group):
            dest = lax.rem(my_group + steps - t, steps) * group + e

            @pl.when(dest != me)
            def _():
                in_copy(2, dest, me).start()
                in_copy(3, dest, me).start()

        return c

    lax.fori_loop(0, steps, send_qg, 0)

    xf[...] = jnp.zeros_like(xf)
    xf[pl.ds(0, txt), :] = x_ref[...].astype(F32)
    whole_x = xf[...]
    for p in range(ndp):
        xs[p] = whole_x[:, p * dloc:(p + 1) * dloc].astype(BF)
    for i in range(1, ndp):
        x_copy(lax.rem(dp + i, ndp), dp).start()
    xall[dp] = xs[dp]
    gf[...] = jnp.zeros_like(gf)
    gf[pl.ds(0, txt), :] = gt_ref[...].astype(F32)

    for i in range(ndp):
        s = lax.rem(dp + i, ndp)
        if i:
            x_copy(dp, s).wait_recv()
        for j in range(3):
            product = dotf(xall[s], w_ref[j])
            if i:
                part[s, j] = product
            else:
                partl[dp, j] = product
        if i:
            p_copy(s, dp).start()
    for i in range(1, ndp):
        p_copy(dp, lax.rem(dp + i, ndp)).wait_recv()
    for j, buf in enumerate((qbuf, kbuf, vbuf)):
        value = partl[0, j]
        for s in range(1, ndp):
            value = value + partl[s, j]
        buf[pl.ds(img, tsub), :] = value.astype(BF)
        pad = buf.shape[0] - img - tsub
        buf[pl.ds(img + tsub, pad), :] = jnp.zeros((pad, cols), BF)
    gbuf[pl.ds(img, tsub), :] = gf[...].astype(BF)
    pad = gbuf.shape[0] - img - tsub
    gbuf[pl.ds(img + tsub, pad), :] = jnp.zeros((pad, cols), BF)
    dkacc[...] = jnp.zeros_like(dkacc)
    dvacc[...] = jnp.zeros_like(dvacc)

    def wait_kv(i, c):
        source = lax.rem(me + i, n)
        in_copy(0, me, source).wait_recv()
        in_copy(1, me, source).wait_recv()
        return c

    lax.fori_loop(1, n, wait_kv, 0)
    for a in range(4):
        own_copy(a).wait()

    lane_head = lax.broadcasted_iota(jnp.int32, (m, cols), 1) // HEAD_DIM

    def build(r, c):
        at = pl.ds(pl.multiple_of(r * 128, 128), 128)
        lane = lax.broadcasted_iota(jnp.int32, (128, cols), 1)
        row = lax.broadcasted_iota(jnp.int32, (128, cols), 0) + r * 128
        kk = kbuf[at, :]
        vv = vbuf[at, :]
        bias = jnp.where((row >= img + txt) & (lane == 0), -1e30, 0.0).astype(BF)
        ones = jnp.ones((128, cols), BF)
        zero = jnp.zeros((128, cols), BF)
        kaug[at, :] = jnp.concatenate([kk, bias], axis=1)
        vaug[at, :] = jnp.concatenate([vv, ones], axis=1)
        for h in range(heads):
            mine = lane // HEAD_DIM == h
            kh[h, at, :] = jnp.where(mine, kk, zero)
            vh[h, at, :] = jnp.concatenate(
                [jnp.where(mine, vv, zero), jnp.where(mine, ones, zero)], axis=1
            )
        return c

    lax.fori_loop(0, length // 128, build, 0)
    scale = 1.0 / math.sqrt(HEAD_DIM)

    def out_copy(a, dest, source):
        send = (obuf, dqbuf, dkb, dvb)[a]
        land = o_out if a == 0 else gr_out.at[a - 1]
        return pltpu.make_async_remote_copy(
            src_ref=at_rows(send, dest), dst_ref=tile(land, source),
            send_sem=out_send.at[a, dest], recv_sem=out_recv.at[a, source],
            device_id={"seq": dest}, device_id_type=pl.DeviceIdType.MESH,
        )

    def own_out(a):
        send = (obuf, dqbuf, dkb, dvb)[a]
        land = o_out if a == 0 else gr_out.at[a - 1]
        return pltpu.make_async_copy(at_rows(send, me), tile(land, me), loc_sem.at[5 + a])

    def step(t, c):
        which = lax.rem(my_group + t + steps - 1, steps)
        first = jnp.where(t == 0, img, which * m)
        for e in range(group):
            source = which * group + e

            @pl.when((t > 0) & (source != me))
            def _():
                in_copy(2, me, source).wait_recv()
                in_copy(3, me, source).wait_recv()

        at = pl.ds(pl.multiple_of(first, 128), m)
        qs = qbuf[at, :] * jnp.asarray(scale, BF)
        g = gbuf[at, :].astype(F32)
        zero = jnp.zeros_like(qs)
        one = jnp.where(lax.broadcasted_iota(jnp.int32, (m, cols), 1) == 0, 1.0, 0.0).astype(BF)
        acc = jnp.zeros((m, 2 * cols), F32)
        for h in range(heads):
            qm = jnp.where(lane_head == h, qs, zero)
            qst[pl.ds(h * m, m), :] = qm
            scores = dotf(jnp.concatenate([qm, one], axis=1), kaug[...], NT)
            top = jnp.max(scores, axis=1, keepdims=True)
            p = jnp.exp(scores - top).astype(BF)
            pbuf[pl.ds(h * m, m), :] = p
            acc = acc + dotf(p, vh[h])
        inverse = 1.0 / acc[:, cols:]
        ob = (acc[:, :cols] * inverse).astype(BF)
        gp = (g * inverse).astype(BF)
        term = -(ob.astype(F32) * gp.astype(F32)).astype(BF)
        dq = jnp.zeros((m, cols), F32)
        for h in range(heads):
            gm = jnp.where(lane_head == h, gp, zero)
            gst[pl.ds(h * m, m), :] = gm
            lhs = jnp.concatenate([gm, jnp.where(lane_head == h, term, zero)], axis=1)
            inner = dotf(lhs, vaug[...], NT)
            ds = inner.astype(BF) * pbuf[pl.ds(h * m, m), :]
            sbuf[pl.ds(h * m, m), :] = ds
            dq = dq + dotf(ds, kh[h])
        obuf[at, :] = ob
        dqbuf[at, :] = (dq * scale).astype(BF)
        for e in range(group):
            dest = which * group + e

            @pl.when((t > 0) & (dest != me))
            def _():
                out_copy(0, dest, me).start()
                out_copy(1, dest, me).start()

            @pl.when((t > 0) & (dest == me))
            def _():
                own_out(0).start()
                own_out(1).start()

        dvacc[...] += dotf(pbuf[...], gst[...], TN)
        dkacc[...] += dotf(sbuf[...], qst[...], TN)
        return c

    lax.fori_loop(0, steps + 1, step, 0)

    text = pl.ds(img, tsub)
    tg[0] = dqbuf[text, :]
    tg[1] = dkacc[text, :].astype(BF)
    tg[2] = dvacc[text, :].astype(BF)
    for i in range(1, ndp):
        t_copy(lax.rem(dp + i, ndp), dp).start()
    ot_out[...] = obuf[text, :].astype(F32)[:txt].astype(BF)

    def send_dkv(i, c):
        dest = lax.rem(me + i, n)
        at = pl.ds(pl.multiple_of(dest * rows, 16), rows)
        dkb[at, :] = dkacc[at, :].astype(BF)
        dvb[at, :] = dvacc[at, :].astype(BF)

        @pl.when(dest != me)
        def _():
            out_copy(2, dest, me).start()
            out_copy(3, dest, me).start()

        @pl.when(dest == me)
        def _():
            own_out(2).start()
            own_out(3).start()

        return c

    lax.fori_loop(1, n + 1, send_dkv, 0)

    tgl[dp] = tg[...]
    for i in range(1, ndp):
        t_copy(dp, lax.rem(dp + i, ndp)).wait_recv()

    part_of = lax.rem(me, QUAD)
    base = me - part_of
    slot = me // QUAD
    per = nb // QUAD

    def d1_copy(e, source):
        return pltpu.make_async_remote_copy(
            src_ref=dxs.at[e], dst_ref=dx1.at[source],
            send_sem=d1s_sem.at[e], recv_sem=d1r_sem.at[source],
            device_id={"seq": base + e}, device_id_type=pl.DeviceIdType.MESH,
        )

    def d2_copy(k, source):
        owner = dp * nb + (k % per) * QUAD + part_of
        return pltpu.make_async_remote_copy(
            src_ref=dx2.at[k], dst_ref=dxl.at[source],
            send_sem=ds_sem.at[k], recv_sem=dr_sem.at[source],
            device_id={"dp": k // per, "seq": owner}, device_id_type=pl.DeviceIdType.MESH,
        )

    def d2_own(k):
        return pltpu.make_async_copy(dx2.at[k], dxl.at[slot], dr_sem.at[slot])

    def is_own(k):
        return (dp == k // per) & (dp * nb + (k % per) * QUAD + part_of == me)

    for s in range(ndp):
        value = dotf(w_ref[0], tgl[s, 0], NT)
        for j in range(1, 3):
            value = value + dotf(w_ref[j], tgl[s, j], NT)
        for b in range(nb):
            dxs[b % QUAD, s * per + b // QUAD] = value[b * dblk:(b + 1) * dblk, :].astype(BF)
    for i in range(1, QUAD):
        d1_copy(lax.rem(part_of + i, QUAD), part_of).start()
    x_out[...] = xall[...]
    tg_out[...] = tgl[...]
    for i in range(1, QUAD):
        d1_copy(part_of, lax.rem(part_of + i, QUAD)).wait_recv()
    for k in range(ndp * per):
        sums = dxs[part_of, k].astype(F32)
        for i in range(1, QUAD):
            sums = sums + dx1[lax.rem(part_of + i, QUAD), k].astype(F32)
        dx2[k] = sums.astype(BF)
    for k in range(ndp * per):

        @pl.when(jnp.logical_not(is_own(k)))
        def _():
            d2_copy(k, slot).start()

        @pl.when(is_own(k))
        def _():
            d2_own(k).start()

    local_dx = me // nb == dp
    for r in range(n // QUAD):

        @pl.when(jnp.logical_not(local_dx & (slot == r)))
        def _():
            d2_copy(0, r).wait_recv()

        @pl.when(local_dx & (slot == r))
        def _():
            d2_own(0).wait()

    sums = dxl[0].astype(F32)
    for r in range(1, n // QUAD):
        sums = sums + dxl[r].astype(F32)
    dx_out[...] = sums[:, :txt]

    for a in range(4):
        own_out(a).wait()

    def drain(i, c):
        other = lax.rem(me + i, n)
        for a in range(4):
            out_copy(a, me, other).wait_recv()
            out_copy(a, other, me).wait_send()
            in_copy(a, other, me).wait_send()
        return c

    lax.fori_loop(1, n, drain, 0)
    for i in range(1, ndp):
        p = lax.rem(dp + i, ndp)
        x_copy(p, dp).wait_send()
        p_copy(p, dp).wait_send()
        t_copy(p, dp).wait_send()
    for i in range(1, QUAD):
        d1_copy(lax.rem(part_of + i, QUAD), part_of).wait_send()
    for k in range(ndp * per):

        @pl.when(jnp.logical_not(is_own(k)))
        def _():
            d2_copy(k, slot).wait_send()


def finish(o_in, gr_in, ot_in, dx_in, x_ref, tg_ref, o_out, gr_out, ot_out, dx_out, dw_out, hold, dwb, in_sem, out_sem):
    def fetch(i):
        return pltpu.make_async_copy(o_in if i == 0 else gr_in.at[i - 1], hold.at[i], in_sem.at[i])

    def put(i):
        return pltpu.make_async_copy(hold.at[i], o_out if i == 0 else gr_out.at[i - 1], out_sem.at[i])

    def put_dw(j):
        return pltpu.make_async_copy(dwb.at[j], dw_out.at[j], out_sem.at[4 + j])

    for i in range(4):
        fetch(i).start()
    ot_out[...] = ot_in[...]
    dx_out[...] = dx_in[...]
    for i in range(4):
        fetch(i).wait()
        put(i).start()
        if i < 3:
            value = dotf(x_ref[0], tg_ref[0, i], TN)
            for s in range(1, x_ref.shape[0]):
                value = value + dotf(x_ref[s], tg_ref[s, i], TN)
            dwb[i] = value
            put_dw(i).start()
    for i in range(4):
        put(i).wait()
    for j in range(3):
        put_dw(j).wait()


def local(n, ndp, q_img, k_img, v_img, x_txt, w_txt, grad_img, grad_txt):
    _, rows, hd = q_img.shape
    cols = hd // n
    heads = cols // HEAD_DIM
    txt, width = x_txt.shape[1:]
    dloc = w_txt.shape[1]
    dblk = width // n
    tsub = up(txt, 16)
    tkey = up(txt, 128)
    group = 2
    m = group * rows
    nb = dloc // dblk
    length = n * rows + tkey
    qlen = n * rows + m
    wide = cols % 128 == 0

    def spread(a):
        return a[0] if wide else a[0].reshape(rows, n, cols).transpose(1, 0, 2)

    shape = (rows, hd) if wide else (n, rows, cols)
    hbm = pl.BlockSpec(memory_space=pl.ANY)
    vmem = pl.BlockSpec(memory_space=pltpu.VMEM)
    cfg = (n, ndp, rows, cols, txt, tsub, tkey, dloc, dblk, group)
    dma = pltpu.SemaphoreType.DMA
    assert nb % QUAD == 0 and n % QUAD == 0
    o, gr, ot, dx, xa, tga = pl.pallas_call(
        functools.partial(kernel, cfg),
        out_shape=(
            jax.ShapeDtypeStruct(shape, BF),
            jax.ShapeDtypeStruct((3,) + shape, BF),
            jax.ShapeDtypeStruct((txt, cols), BF),
            jax.ShapeDtypeStruct((dblk, txt), F32),
            jax.ShapeDtypeStruct((ndp, tsub, dloc), BF),
            jax.ShapeDtypeStruct((ndp, 3, tsub, cols), BF),
        ),
        in_specs=[hbm] * 4 + [vmem] * 3,
        out_specs=(hbm, hbm, vmem, vmem, vmem, vmem),
        scratch_shapes=[
            pltpu.VMEM((length, cols), BF),
            pltpu.VMEM((length, cols), BF),
            pltpu.VMEM((qlen, cols), BF),
            pltpu.VMEM((qlen, cols), BF),
            pltpu.VMEM((ndp, tsub, dloc), BF),
            pltpu.VMEM((ndp, 3, tsub, cols), F32),
            pltpu.VMEM((ndp, 3, tsub, cols), F32),
            pltpu.VMEM((length, 2 * cols), BF),
            pltpu.VMEM((heads, length, cols), BF),
            pltpu.VMEM((length, 2 * cols), BF),
            pltpu.VMEM((heads, length, 2 * cols), BF),
            pltpu.VMEM((heads * m, length), BF),
            pltpu.VMEM((heads * m, length), BF),
            pltpu.VMEM((heads * m, cols), BF),
            pltpu.VMEM((heads * m, cols), BF),
            pltpu.VMEM((qlen, cols), BF),
            pltpu.VMEM((qlen, cols), BF),
            pltpu.VMEM((length, cols), F32),
            pltpu.VMEM((length, cols), F32),
            pltpu.VMEM((length, cols), BF),
            pltpu.VMEM((length, cols), BF),
            pltpu.VMEM((3, tsub, cols), BF),
            pltpu.VMEM((ndp, 3, tsub, cols), BF),
            pltpu.VMEM((QUAD, ndp * nb // QUAD, dblk, tsub), BF),
            pltpu.VMEM((QUAD, ndp * nb // QUAD, dblk, tsub), BF),
            pltpu.VMEM((ndp * nb // QUAD, dblk, tsub), BF),
            pltpu.VMEM((n // QUAD, dblk, tsub), BF),
            pltpu.VMEM((tsub, width), F32),
            pltpu.VMEM((tsub, cols), F32),
            pltpu.VMEM((ndp, tsub, dloc), BF),
            dma((4, n)), dma((4, n)), dma((4, n)), dma((4, n)),
            dma((ndp,)), dma((ndp,)), dma((ndp,)), dma((ndp,)), dma((ndp,)), dma((ndp,)),
            dma((QUAD,)), dma((QUAD,)), dma((ndp * nb // QUAD,)), dma((n // QUAD,)), dma((9,)),
        ],
        compiler_params=pltpu.CompilerParams(
            collective_id=0, has_side_effects=True, vmem_limit_bytes=60 * 1024 * 1024
        ),
    )(spread(q_img), spread(k_img), spread(v_img), spread(grad_img), x_txt[0], w_txt, grad_txt[0])
    o, gr, ot, dx, dw = pl.pallas_call(
        finish,
        out_shape=(
            jax.ShapeDtypeStruct(shape, BF),
            jax.ShapeDtypeStruct((3,) + shape, BF),
            jax.ShapeDtypeStruct((txt, cols), BF),
            jax.ShapeDtypeStruct((dblk, txt), F32),
            jax.ShapeDtypeStruct((3, dloc, cols), F32),
        ),
        in_specs=[hbm] * 2 + [vmem] * 4,
        out_specs=(hbm, hbm, vmem, vmem, hbm),
        scratch_shapes=[
            pltpu.VMEM((4,) + shape, BF), pltpu.VMEM((3, dloc, cols), F32), dma((4,)), dma((7,)),
        ],
    )(o, gr, ot, dx, xa, tga)
    if not wide:
        o = o.transpose(1, 0, 2).reshape(rows, hd)
        gr = gr.transpose(0, 2, 1, 3).reshape(3, rows, hd)
    return (o[None], ot[None], gr[:, None], dx.T[None], dw)


def solution(mesh):
    n, ndp = mesh.shape["seq"], mesh.shape["dp"]
    in_specs = (
        P("dp", "seq", None),
        P("dp", "seq", None),
        P("dp", "seq", None),
        P("dp", None, None),
        P(None, "dp", "seq"),
        P("dp", "seq", None),
        P("dp", None, "seq"),
    )
    out_specs = (
        P("dp", "seq", None),
        P("dp", None, "seq"),
        P(None, "dp", "seq", None),
        P("dp", None, "seq"),
        P(None, "dp", "seq"),
    )
    return jax.shard_map(
        functools.partial(local, n, ndp), mesh=mesh, in_specs=in_specs, out_specs=out_specs,
        check_vma=False,
    )
```

```python
import functools
import math

import jax
import jax.numpy as jnp
from jax import lax
from jax.experimental import pallas as pl
from jax.experimental.pallas import tpu as pltpu
from jax.sharding import PartitionSpec as P

HEAD_DIM = 64
QUAD = 4
BF = jnp.bfloat16
F32 = jnp.float32
NT = (((1,), (1,)), ((), ()))
TN = (((0,), (0,)), ((), ()))


def up(value, step):
    return (value + step - 1) // step * step


def dotf(a, b, dims=(((1,), (0,)), ((), ()))):
    return lax.dot_general(a, b, dims, preferred_element_type=F32)


def kernel(
    cfg,
    q_in, k_in, v_in, g_in, x_ref, w_ref, gt_ref,
    o_out, gr_out, ot_out, dx_out, x_out, tg_out,
    kbuf, vbuf, qbuf, gbuf, xall, part, partl, kaug, kh, vaug, vh, pbuf, sbuf, gst, qst,
    obuf, dqbuf, dkacc, dvacc, dkb, dvb, tg, tgl, dxs, dx1, dx2, dxl,
    xf, gf, xs,
    in_send, in_recv, out_send, out_recv, xs_sem, xr_sem, ps_sem, pr_sem, ts_sem, tr_sem,
    d1s_sem, d1r_sem, ds_sem, dr_sem, loc_sem,
):
    n, ndp, rows, cols, txt, tsub, tkey, dloc, dblk, group = cfg
    heads = cols // HEAD_DIM
    img = n * rows
    length = img + tkey
    m = group * rows
    steps = n // group
    nb = dloc // dblk
    me = lax.axis_index("seq")
    dp = lax.axis_index("dp")
    wide = cols % 128 == 0

    def tile(ref, j):
        if wide:
            return ref.at[:, pl.ds(pl.multiple_of(j * cols, 128), cols)]
        return ref.at[j]

    def at_rows(ref, j):
        return ref.at[pl.ds(pl.multiple_of(j * rows, 16), rows), :]

    barrier = pltpu.get_barrier_semaphore()
    total = n * ndp

    def greet(i, c):
        flat = lax.rem(dp * n + me + i, total)
        pl.semaphore_signal(
            barrier, inc=1, device_id={"dp": flat // n, "seq": lax.rem(flat, n)},
            device_id_type=pl.DeviceIdType.MESH,
        )
        return c

    lax.fori_loop(1, total, greet, 0)
    pl.semaphore_wait(barrier, total - 1)

    ins = (k_in, v_in, q_in, g_in)
    bufs = (kbuf, vbuf, qbuf, gbuf)

    def in_copy(a, dest, source):
        return pltpu.make_async_remote_copy(
            src_ref=tile(ins[a], dest), dst_ref=at_rows(bufs[a], source),
            send_sem=in_send.at[a, dest], recv_sem=in_recv.at[a, source],
            device_id={"seq": dest}, device_id_type=pl.DeviceIdType.MESH,
        )

    def own_copy(a):
        return pltpu.make_async_copy(tile(ins[a], me), at_rows(bufs[a], me), loc_sem.at[a])

    def x_copy(p, source):
        return pltpu.make_async_remote_copy(
            src_ref=xs.at[p], dst_ref=xall.at[source],
            send_sem=xs_sem.at[p], recv_sem=xr_sem.at[source],
            device_id={"dp": p}, device_id_type=pl.DeviceIdType.MESH,
        )

    def p_copy(p, source):
        return pltpu.make_async_remote_copy(
            src_ref=part.at[p], dst_ref=partl.at[source],
            send_sem=ps_sem.at[p], recv_sem=pr_sem.at[source],
            device_id={"dp": p}, device_id_type=pl.DeviceIdType.MESH,
        )

    def t_copy(p, source):
        return pltpu.make_async_remote_copy(
            src_ref=tg, dst_ref=tgl.at[source],
            send_sem=ts_sem.at[p], recv_sem=tr_sem.at[source],
            device_id={"dp": p}, device_id_type=pl.DeviceIdType.MESH,
        )

    my_group = me // group

    def partner(t):
        value, bit = 0, 1
        while bit < steps:
            value = value + bit * lax.rem(my_group // bit + t // bit, 2)
            bit *= 2
        return value

    def send_kv(t, c):
        for e in range(group):
            dest = partner(t) * group + e

            @pl.when(dest != me)
            def _():
                in_copy(0, dest, me).start()
                in_copy(1, dest, me).start()

        return c

    xf[...] = jnp.zeros_like(xf)
    xf[pl.ds(0, txt), :] = x_ref[...].astype(F32)
    whole_x = xf[...]
    for p in range(ndp):
        xs[p] = whole_x[:, p * dloc:(p + 1) * dloc].astype(BF)
    for i in range(1, ndp):
        x_copy(lax.rem(dp + i, ndp), dp).start()
    lax.fori_loop(0, steps, send_kv, 0)
    for a in range(4):
        own_copy(a).start()

    def send_qg(t, c):
        for e in range(group):
            dest = partner(t) * group + e

            @pl.when(dest != me)
            def _():
                in_copy(2, dest, me).start()
                in_copy(3, dest, me).start()

        return c

    xall[dp] = xs[dp]
    gf[...] = jnp.zeros_like(gf)
    gf[pl.ds(0, txt), :] = gt_ref[...].astype(F32)

    for i in range(ndp):
        s = lax.rem(dp + i, ndp)
        if i:
            x_copy(dp, s).wait_recv()
        for j in range(3):
            product = dotf(xall[s], w_ref[j])
            if i:
                part[s, j] = product
            else:
                partl[dp, j] = product
        if i:
            p_copy(s, dp).start()
    for i in range(1, ndp):
        p_copy(dp, lax.rem(dp + i, ndp)).wait_recv()
    for j, buf in enumerate((qbuf, kbuf, vbuf)):
        value = partl[0, j]
        for s in range(1, ndp):
            value = value + partl[s, j]
        buf[pl.ds(img, tsub), :] = value.astype(BF)
        pad = buf.shape[0] - img - tsub
        buf[pl.ds(img + tsub, pad), :] = jnp.zeros((pad, cols), BF)
    gbuf[pl.ds(img, tsub), :] = gf[...].astype(BF)
    pad = gbuf.shape[0] - img - tsub
    gbuf[pl.ds(img + tsub, pad), :] = jnp.zeros((pad, cols), BF)
    dkacc[...] = jnp.zeros_like(dkacc)
    dvacc[...] = jnp.zeros_like(dvacc)

    for a in range(4):
        own_copy(a).wait()
    def build(first, count):
        at = pl.ds(first if isinstance(first, int) else pl.multiple_of(first, 128), count)
        lane = lax.broadcasted_iota(jnp.int32, (count, cols), 1)
        row = lax.broadcasted_iota(jnp.int32, (count, cols), 0) + first
        kk = kbuf[at, :]
        vv = vbuf[at, :]
        bias = jnp.where((row >= img + txt) & (lane == 0), -1e30, 0.0).astype(BF)
        ones = jnp.ones((count, cols), BF)
        zero = jnp.zeros((count, cols), BF)
        kaug[at, :] = jnp.concatenate([kk, bias], axis=1)
        vaug[at, :] = jnp.concatenate([vv, ones], axis=1)
        for h in range(heads):
            mine = lane // HEAD_DIM == h
            kh[h, at, :] = jnp.where(mine, kk, zero)
            vh[h, at, :] = jnp.concatenate(
                [jnp.where(mine, vv, zero), jnp.where(mine, ones, zero)], axis=1
            )

    build(img, tkey)

    def wait_kv(t, c):
        for e in range(group):
            source = partner(t) * group + e

            @pl.when(source != me)
            def _():
                in_copy(0, me, source).wait_recv()
                in_copy(1, me, source).wait_recv()

            build(source * rows, rows)
        return c

    lax.fori_loop(0, steps, wait_kv, 0)
    lax.fori_loop(0, steps, send_qg, 0)
    scale = 1.0 / math.sqrt(HEAD_DIM)

    def out_copy(a, dest, source):
        send = (obuf, dqbuf, dkb, dvb)[a]
        land = o_out if a == 0 else gr_out.at[a - 1]
        return pltpu.make_async_remote_copy(
            src_ref=at_rows(send, dest), dst_ref=tile(land, source),
            send_sem=out_send.at[a, dest], recv_sem=out_recv.at[a, source],
            device_id={"seq": dest}, device_id_type=pl.DeviceIdType.MESH,
        )

    def own_out(a):
        send = (obuf, dqbuf, dkb, dvb)[a]
        land = o_out if a == 0 else gr_out.at[a - 1]
        return pltpu.make_async_copy(at_rows(send, me), tile(land, me), loc_sem.at[5 + a])

    def attend(first, m):
        at = pl.ds(first if isinstance(first, int) else pl.multiple_of(first, 128), m)
        lane_head = lax.broadcasted_iota(jnp.int32, (m, cols), 1) // HEAD_DIM
        qs = qbuf[at, :] * jnp.asarray(scale, BF)
        g = gbuf[at, :].astype(F32)
        zero = jnp.zeros_like(qs)
        one = jnp.where(lax.broadcasted_iota(jnp.int32, (m, cols), 1) == 0, 1.0, 0.0).astype(BF)
        acc = jnp.zeros((m, 2 * cols), F32)
        for h in range(heads):
            qm = jnp.where(lane_head == h, qs, zero)
            qst[pl.ds(h * m, m), :] = qm
            scores = dotf(jnp.concatenate([qm, one], axis=1), kaug[...], NT)
            top = jnp.max(scores, axis=1, keepdims=True)
            p = jnp.exp(scores - top).astype(BF)
            pbuf[pl.ds(h * m, m), :] = p
            acc = acc + dotf(p, vh[h])
        inverse = 1.0 / acc[:, cols:]
        ob = (acc[:, :cols] * inverse).astype(BF)
        gp = (g * inverse).astype(BF)
        term = -(ob.astype(F32) * gp.astype(F32)).astype(BF)
        dq = jnp.zeros((m, cols), F32)
        for h in range(heads):
            gm = jnp.where(lane_head == h, gp, zero)
            gst[pl.ds(h * m, m), :] = gm
            lhs = jnp.concatenate([gm, jnp.where(lane_head == h, term, zero)], axis=1)
            inner = dotf(lhs, vaug[...], NT)
            ds = inner.astype(BF) * pbuf[pl.ds(h * m, m), :]
            sbuf[pl.ds(h * m, m), :] = ds
            dq = dq + dotf(ds, kh[h])
        obuf[at, :] = ob
        dqbuf[at, :] = (dq * scale).astype(BF)

    def accumulate(m):
        stacked = pl.ds(0, heads * m)
        dvacc[...] += dotf(pbuf[stacked, :], gst[stacked, :], TN)
        dkacc[...] += dotf(sbuf[stacked, :], qst[stacked, :], TN)

    attend(img, tkey)
    accumulate(tkey)

    def step(t, c):
        which = partner(t)
        for e in range(group):
            source = which * group + e

            @pl.when(source != me)
            def _():
                in_copy(2, me, source).wait_recv()
                in_copy(3, me, source).wait_recv()

        attend(which * m, m)
        for e in range(group):
            dest = which * group + e

            @pl.when(dest != me)
            def _():
                out_copy(0, dest, me).start()
                out_copy(1, dest, me).start()

            @pl.when(dest == me)
            def _():
                own_out(0).start()
                own_out(1).start()

        accumulate(m)
        return c

    lax.fori_loop(0, steps, step, 0)

    text = pl.ds(img, tsub)
    tg[0] = dqbuf[text, :]
    tg[1] = dkacc[text, :].astype(BF)
    tg[2] = dvacc[text, :].astype(BF)
    for i in range(1, ndp):
        t_copy(lax.rem(dp + i, ndp), dp).start()
    ot_out[...] = obuf[text, :].astype(F32)[:txt].astype(BF)

    def send_dkv(t, c):
        for e in range(group):
            dest = partner(t) * group + e
            at = pl.ds(pl.multiple_of(dest * rows, 16), rows)
            dkb[at, :] = dkacc[at, :].astype(BF)
            dvb[at, :] = dvacc[at, :].astype(BF)

            @pl.when(dest != me)
            def _():
                out_copy(2, dest, me).start()
                out_copy(3, dest, me).start()

            @pl.when(dest == me)
            def _():
                own_out(2).start()
                own_out(3).start()

        return c

    near = QUAD // group
    lax.fori_loop(near, steps, send_dkv, 0)

    tgl[dp] = tg[...]
    for i in range(1, ndp):
        t_copy(dp, lax.rem(dp + i, ndp)).wait_recv()

    part_of = lax.rem(me, QUAD)
    base = me - part_of
    slot = me // QUAD
    per = nb // QUAD

    def d1_copy(e, source):
        return pltpu.make_async_remote_copy(
            src_ref=dxs.at[e], dst_ref=dx1.at[source],
            send_sem=d1s_sem.at[e], recv_sem=d1r_sem.at[source],
            device_id={"seq": base + e}, device_id_type=pl.DeviceIdType.MESH,
        )

    def d2_copy(k, source):
        owner = dp * nb + (k % per) * QUAD + part_of
        return pltpu.make_async_remote_copy(
            src_ref=dx2.at[k], dst_ref=dxl.at[source],
            send_sem=ds_sem.at[k], recv_sem=dr_sem.at[source],
            device_id={"dp": k // per, "seq": owner}, device_id_type=pl.DeviceIdType.MESH,
        )

    def d2_own(k):
        return pltpu.make_async_copy(dx2.at[k], dxl.at[slot], dr_sem.at[slot])

    def is_own(k):
        return (dp == k // per) & (dp * nb + (k % per) * QUAD + part_of == me)

    for s in range(ndp):
        value = dotf(w_ref[0], tgl[s, 0], NT)
        for j in range(1, 3):
            value = value + dotf(w_ref[j], tgl[s, j], NT)
        for b in range(nb):
            dxs[b % QUAD, s * per + b // QUAD] = value[b * dblk:(b + 1) * dblk, :].astype(BF)
    for i in range(1, QUAD):
        d1_copy(lax.rem(part_of + i, QUAD), part_of).start()
    lax.fori_loop(0, near, send_dkv, 0)
    x_out[...] = xall[...]
    tg_out[...] = tgl[...]
    for i in range(1, QUAD):
        d1_copy(part_of, lax.rem(part_of + i, QUAD)).wait_recv()
    for k in range(ndp * per):
        sums = dxs[part_of, k].astype(F32)
        for i in range(1, QUAD):
            sums = sums + dx1[lax.rem(part_of + i, QUAD), k].astype(F32)
        dx2[k] = sums.astype(BF)
    for k in range(ndp * per):

        @pl.when(jnp.logical_not(is_own(k)))
        def _():
            d2_copy(k, slot).start()

        @pl.when(is_own(k))
        def _():
            d2_own(k).start()

    local_dx = me // nb == dp
    for r in range(n // QUAD):

        @pl.when(jnp.logical_not(local_dx & (slot == r)))
        def _():
            d2_copy(0, r).wait_recv()

        @pl.when(local_dx & (slot == r))
        def _():
            d2_own(0).wait()

    sums = dxl[0].astype(F32)
    for r in range(1, n // QUAD):
        sums = sums + dxl[r].astype(F32)
    dx_out[...] = sums[:, :txt]

    for a in range(4):
        own_out(a).wait()

    def drain(i, c):
        other = lax.rem(me + i, n)
        for a in range(4):
            out_copy(a, me, other).wait_recv()
            out_copy(a, other, me).wait_send()
            in_copy(a, other, me).wait_send()
        return c

    lax.fori_loop(1, n, drain, 0)
    for i in range(1, ndp):
        p = lax.rem(dp + i, ndp)
        x_copy(p, dp).wait_send()
        p_copy(p, dp).wait_send()
        t_copy(p, dp).wait_send()
    for i in range(1, QUAD):
        d1_copy(lax.rem(part_of + i, QUAD), part_of).wait_send()
    for k in range(ndp * per):

        @pl.when(jnp.logical_not(is_own(k)))
        def _():
            d2_copy(k, slot).wait_send()


def finish(o_in, gr_in, ot_in, dx_in, x_ref, tg_ref, o_out, gr_out, ot_out, dx_out, dw_out, hold, dwb, in_sem, out_sem):
    def fetch(i):
        return pltpu.make_async_copy(o_in if i == 0 else gr_in.at[i - 1], hold.at[i], in_sem.at[i])

    def put(i):
        return pltpu.make_async_copy(hold.at[i], o_out if i == 0 else gr_out.at[i - 1], out_sem.at[i])

    def put_dw(j):
        return pltpu.make_async_copy(dwb.at[j], dw_out.at[j], out_sem.at[4 + j])

    for i in range(4):
        fetch(i).start()
    ot_out[...] = ot_in[...]
    dx_out[...] = dx_in[...]
    for i in range(4):
        fetch(i).wait()
        put(i).start()
    for i in range(3):
        value = dotf(x_ref[0], tg_ref[0, i], TN)
        for s in range(1, x_ref.shape[0]):
            value = value + dotf(x_ref[s], tg_ref[s, i], TN)
        dwb[i] = value
        put_dw(i).start()
    for i in range(4):
        put(i).wait()
    for j in range(3):
        put_dw(j).wait()


def local(n, ndp, q_img, k_img, v_img, x_txt, w_txt, grad_img, grad_txt):
    _, rows, hd = q_img.shape
    cols = hd // n
    heads = cols // HEAD_DIM
    txt, width = x_txt.shape[1:]
    dloc = w_txt.shape[1]
    dblk = width // n
    tsub = up(txt, 16)
    tkey = up(txt, 128)
    group = 2
    m = group * rows
    nb = dloc // dblk
    length = n * rows + tkey
    qlen = n * rows + m
    wide = cols % 128 == 0

    def spread(a):
        return a[0] if wide else a[0].reshape(rows, n, cols).transpose(1, 0, 2)

    shape = (rows, hd) if wide else (n, rows, cols)
    hbm = pl.BlockSpec(memory_space=pl.ANY)
    vmem = pl.BlockSpec(memory_space=pltpu.VMEM)
    cfg = (n, ndp, rows, cols, txt, tsub, tkey, dloc, dblk, group)
    dma = pltpu.SemaphoreType.DMA
    steps = n // group
    assert nb % QUAD == 0 and n % QUAD == 0 and steps & (steps - 1) == 0
    o, gr, ot, dx, xa, tga = pl.pallas_call(
        functools.partial(kernel, cfg),
        out_shape=(
            jax.ShapeDtypeStruct(shape, BF),
            jax.ShapeDtypeStruct((3,) + shape, BF),
            jax.ShapeDtypeStruct((txt, cols), BF),
            jax.ShapeDtypeStruct((dblk, txt), F32),
            jax.ShapeDtypeStruct((ndp, tsub, dloc), BF),
            jax.ShapeDtypeStruct((ndp, 3, tsub, cols), BF),
        ),
        in_specs=[hbm] * 4 + [vmem] * 3,
        out_specs=(hbm, hbm, vmem, vmem, vmem, vmem),
        scratch_shapes=[
            pltpu.VMEM((length, cols), BF),
            pltpu.VMEM((length, cols), BF),
            pltpu.VMEM((qlen, cols), BF),
            pltpu.VMEM((qlen, cols), BF),
            pltpu.VMEM((ndp, tsub, dloc), BF),
            pltpu.VMEM((ndp, 3, tsub, cols), F32),
            pltpu.VMEM((ndp, 3, tsub, cols), F32),
            pltpu.VMEM((length, 2 * cols), BF),
            pltpu.VMEM((heads, length, cols), BF),
            pltpu.VMEM((length, 2 * cols), BF),
            pltpu.VMEM((heads, length, 2 * cols), BF),
            pltpu.VMEM((heads * m, length), BF),
            pltpu.VMEM((heads * m, length), BF),
            pltpu.VMEM((heads * m, cols), BF),
            pltpu.VMEM((heads * m, cols), BF),
            pltpu.VMEM((qlen, cols), BF),
            pltpu.VMEM((qlen, cols), BF),
            pltpu.VMEM((length, cols), F32),
            pltpu.VMEM((length, cols), F32),
            pltpu.VMEM((length, cols), BF),
            pltpu.VMEM((length, cols), BF),
            pltpu.VMEM((3, tsub, cols), BF),
            pltpu.VMEM((ndp, 3, tsub, cols), BF),
            pltpu.VMEM((QUAD, ndp * nb // QUAD, dblk, tsub), BF),
            pltpu.VMEM((QUAD, ndp * nb // QUAD, dblk, tsub), BF),
            pltpu.VMEM((ndp * nb // QUAD, dblk, tsub), BF),
            pltpu.VMEM((n // QUAD, dblk, tsub), BF),
            pltpu.VMEM((tsub, width), F32),
            pltpu.VMEM((tsub, cols), F32),
            pltpu.VMEM((ndp, tsub, dloc), BF),
            dma((4, n)), dma((4, n)), dma((4, n)), dma((4, n)),
            dma((ndp,)), dma((ndp,)), dma((ndp,)), dma((ndp,)), dma((ndp,)), dma((ndp,)),
            dma((QUAD,)), dma((QUAD,)), dma((ndp * nb // QUAD,)), dma((n // QUAD,)), dma((9,)),
        ],
        compiler_params=pltpu.CompilerParams(
            collective_id=0, has_side_effects=True, vmem_limit_bytes=60 * 1024 * 1024
        ),
    )(spread(q_img), spread(k_img), spread(v_img), spread(grad_img), x_txt[0], w_txt, grad_txt[0])
    o, gr, ot, dx, dw = pl.pallas_call(
        finish,
        out_shape=(
            jax.ShapeDtypeStruct(shape, BF),
            jax.ShapeDtypeStruct((3,) + shape, BF),
            jax.ShapeDtypeStruct((txt, cols), BF),
            jax.ShapeDtypeStruct((dblk, txt), F32),
            jax.ShapeDtypeStruct((3, dloc, cols), F32),
        ),
        in_specs=[hbm] * 2 + [vmem] * 4,
        out_specs=(hbm, hbm, vmem, vmem, hbm),
        scratch_shapes=[
            pltpu.VMEM((4,) + shape, BF), pltpu.VMEM((3, dloc, cols), F32), dma((4,)), dma((7,)),
        ],
    )(o, gr, ot, dx, xa, tga)
    if not wide:
        o = o.transpose(1, 0, 2).reshape(rows, hd)
        gr = gr.transpose(0, 2, 1, 3).reshape(3, rows, hd)
    return (o[None], ot[None], gr[:, None], dx.T[None], dw)


def solution(mesh):
    n, ndp = mesh.shape["seq"], mesh.shape["dp"]
    in_specs = (
        P("dp", "seq", None),
        P("dp", "seq", None),
        P("dp", "seq", None),
        P("dp", None, None),
        P(None, "dp", "seq"),
        P("dp", "seq", None),
        P("dp", None, "seq"),
    )
    out_specs = (
        P("dp", "seq", None),
        P("dp", None, "seq"),
        P(None, "dp", "seq", None),
        P("dp", None, "seq"),
        P(None, "dp", "seq"),
    )
    return jax.shard_map(
        functools.partial(local, n, ndp), mesh=mesh, in_specs=in_specs, out_specs=out_specs,
        check_vma=False,
    )
```
